32 devices in a mesh: dp: 16 (over z, x, core), tensor: 2 (over y).
Axes of the slice: x: 2, y: 2, z: 4, core: 2. Of those that a mesh axis runs over, the one named last changes fastest.
Arguments:
- hidden_in: bfloat16 [4096, 1536], P(('dp', 'tensor')), may hold values from -6 to 6
- cotangent: float32 [4096, 1536], P(('dp', 'tensor')), may hold values from -6 to 6
- segments: int32 [16, 256], P('dp'), may hold values from 0 to 3, as said below
- positions: int32 [16, 256], P('dp'), may hold values from 0 to 127, as said below
- norm_gains: bfloat16 [1, 2, 1536], P(None, None, 'dp'), may hold values from 0.099609375 to 1.8984375
- q_weight: bfloat16 [1, 1536, 1536], P(None, 'dp', 'tensor'), may hold values from -0.15625 to 0.15625
- k_weight: bfloat16 [1, 1536, 256], P(None, 'dp', 'tensor'), may hold values from -0.15625 to 0.15625
- v_weight: bfloat16 [1, 1536, 256], P(None, 'dp', 'tensor'), may hold values from -0.15625 to 0.15625
- q_bias: bfloat16 [1, 12, 128], P(None, 'tensor', 'dp'), may hold values from -3 to 3
- k_bias: bfloat16 [1, 2, 128], P(None, 'tensor', 'dp'), may hold values from -3 to 3
- v_bias: bfloat16 [1, 2, 128], P(None, 'tensor', 'dp'), may hold values from -3 to 3
- o_weight: bfloat16 [1, 1536, 1536], P(None, 'tensor', 'dp'), may hold values from -0.625 to 0.625
- gate_weight: bfloat16 [1, 1536, 8960], P(None, 'dp', 'tensor'), may hold values from -0.15625 to 0.15625
- up_weight: bfloat16 [1, 1536, 8960], P(None, 'dp', 'tensor'), may hold values from -0.15625 to 0.15625
- down_weight: bfloat16 [1, 8960, 1536], P(None, 'tensor', 'dp'), may hold values from -0.0625 to 0.0625
Outputs:
- hidden_out: float32 [4096, 1536], P(('dp', 'tensor'))
- input_grad: float32 [4096, 1536], P(('dp', 'tensor'))
- gain_grads: float32 [1, 2, 1536], P(None, None, ('dp', 'tensor'))
- q_weight_grad: float32 [1, 1536, 1536], P(None, 'dp', 'tensor')
- k_weight_grad: float32 [1, 1536, 256], P(None, 'dp', 'tensor')
- v_weight_grad: float32 [1, 1536, 256], P(None, 'dp', 'tensor')
- o_weight_grad: float32 [1, 1536, 1536], P(None, 'tensor', 'dp')
- q_bias_grad: float32 [1, 12, 128], P(None, 'tensor', 'dp')
- k_bias_grad: float32 [1, 2, 128], P(None, 'tensor')
- v_bias_grad: float32 [1, 2, 128], P(None, 'tensor', 'dp')
- gate_weight_grad: float32 [1, 1536, 8960], P(None, 'dp', 'tensor')
- up_weight_grad: float32 [1, 1536, 8960], P(None, 'dp', 'tensor')
- down_weight_grad: float32 [1, 8960, 1536], P(None, 'tensor', 'dp')
The draws below stay inside these ranges and needn't reach their ends.
Inputs may be any that keep to these rules, and one draw needn't show every extreme that they name: `segments`: document numbers never fall along a sequence and rise by one where a document starts; every sequence holds exactly 4 documents, one of them 256 / 2 tokens long. `positions`: A token's position within its document, 0 at the document's first token and rising by one.
All inputs are finite; a program needn't handle non-finite values.
Results may differ from the reference program's by a relative error of at most 0.02.
Values may be sent and summed in bfloat16 or wider, within the bound.
No kernel may reach another device: no remote copies, remote signals or barrier semaphores. Data moves between devices by JAX's collectives and lax.ppermute only.
A program may use at most 256 MiB of HBM per device.

```python
import jax
import jax.numpy as jnp
from jax import lax

D = 1536
H = 12
KV = 2
HD = 128
FF = 8960
LAYERS = 1
SEQ_LEN = 256
SEQS = 16
TOKENS = 4096


def segment_layout(key):
    base_key = jax.random.fold_in(key, 7)
    key_one, key_two, key_three = jax.random.split(base_key, 3)
    quarter = SEQ_LEN // 4
    longest = SEQ_LEN // 2
    first_len = jax.random.randint(key_one, (SEQS,), 1, quarter)
    second_len = jax.random.randint(key_two, (SEQS,), 1, quarter)
    third_len = longest - first_len - second_len
    spot = jax.random.randint(key_three, (SEQS,), 0, 4)
    shorter = jnp.stack([first_len, second_len, third_len], axis=1)
    slots = jnp.arange(4)
    pick = slots[None, :] - (slots[None, :] > spot[:, None]).astype(jnp.int32)
    pick = jnp.clip(pick, 0, 2)
    picked = jnp.sum(shorter[:, None, :] * (pick[:, :, None] == jnp.arange(3)[None, None, :]).astype(jnp.int32), axis=-1)
    lengths = jnp.where(slots[None, :] == spot[:, None], longest, picked)
    ends = jnp.cumsum(lengths, axis=1)
    starts = ends - lengths
    places = jnp.arange(SEQ_LEN)
    seg_ids = jnp.sum((places[None, :, None] >= ends[:, None, :3]).astype(jnp.int32), axis=-1)
    onehot = (seg_ids[:, :, None] == slots[None, None, :]).astype(jnp.int32)
    seg_start = jnp.sum(onehot * starts[:, None, :], axis=-1)
    return (seg_ids.astype(jnp.int32), (places[None, :] - seg_start).astype(jnp.int32))


def draw_segments(key, part):
    return segment_layout(key)[0]


def draw_positions(key, part):
    return segment_layout(key)[1]


def raised(drawn, key, source, target, shards_of, factor):
    def block_of(dim):
        return (jnp.arange(drawn.shape[dim]) // (drawn.shape[dim] // shards_of)).reshape((-1,) + (1,) * (drawn.ndim - 1 - dim))

    first = jax.random.permutation(key, shards_of)[block_of(target)]
    other_side = (block_of(target) + shards_of // 2) % shards_of
    return jnp.where((block_of(source) == first) | (block_of(source) == other_side), factor * drawn, drawn)


def block_levels(key, extent, pieces, low, high):
    factor_of, own = 1.0, jax.random.fold_in(key, 6)
    for dim, shards_of in pieces:
        steps = jnp.exp(jax.random.uniform(jax.random.fold_in(own, dim), (shards_of,), jnp.float32, low / len(pieces), high / len(pieces)))
        factor_of = factor_of * jnp.repeat(steps, extent[dim] // shards_of).reshape([-1 if axis == dim else 1 for axis in range(len(extent))])
    return factor_of


def noise(rng, dims, spread, bound, pieces=(), held_as=jnp.bfloat16):
    entries = spread * jax.random.normal(rng, dims, jnp.float32)
    if pieces:
        entries = entries * block_levels(rng, dims, pieces, -0.22, 0.18)
    return jnp.clip(entries, -bound, bound).astype(held_as)


def gaussian_with(stream_key, shape, width, limit, pieces, heavy, kind=jnp.bfloat16):
    values = width * jax.random.normal(stream_key, shape, jnp.float32)
    if pieces:
        values = values * block_levels(stream_key, shape, pieces, -0.22, 0.18)
    return jnp.clip(raised(values, jax.random.fold_in(stream_key, 3), *heavy), -limit, limit).astype(kind)


def setup_inputs(seed: int = 0) -> dict:
    streams_of = jax.random.split(jax.random.key(seed), 16)
    return {
        "hidden_in": gaussian_with(streams_of[0], (TOKENS, D), 1.0, 6.0, ((0, 32),), (0, 1, 32, 2.75)),
        "cotangent": gaussian_with(streams_of[1], (TOKENS, D), 1.0, 6.0, ((0, 32),), (0, 1, 32, 2.75), jnp.float32),
        "segments": draw_segments(jax.random.fold_in(streams_of[15], 71), 0),
        "positions": draw_positions(jax.random.fold_in(streams_of[15], 71), 0),
        "norm_gains": jnp.clip(1.0 + 0.18 * jax.random.normal(streams_of[4], (LAYERS, 2, D), jnp.float32), 0.099609375, 1.8984375).astype(jnp.bfloat16),
        "q_weight": noise(streams_of[5], (LAYERS, D, H * HD), D ** -0.5, 0.15625, ((1, 16), (2, 2))),
        "k_weight": noise(streams_of[6], (LAYERS, D, KV * HD), D ** -0.5, 0.15625, ((1, 16), (2, 2))),
        "v_weight": noise(streams_of[7], (LAYERS, D, KV * HD), D ** -0.5, 0.15625, ((1, 16), (2, 2))),
        "q_bias": noise(streams_of[8], (LAYERS, H, HD), 0.5, 3.0, ((1, 2), (2, 16))),
        "k_bias": noise(streams_of[9], (LAYERS, KV, HD), 0.5, 3.0, ((1, 2), (2, 16))),
        "v_bias": noise(streams_of[10], (LAYERS, KV, HD), 0.5, 3.0, ((1, 2), (2, 16))),
        "o_weight": noise(streams_of[11], (LAYERS, H * HD, D), (H * HD // 16) ** -0.5, 0.625, ((1, 2), (2, 16))),
        "gate_weight": noise(streams_of[12], (LAYERS, D, FF), D ** -0.5, 0.15625, ((1, 16), (2, 2))),
        "up_weight": noise(streams_of[13], (LAYERS, D, FF), D ** -0.5, 0.15625, ((1, 16), (2, 2))),
        "down_weight": noise(streams_of[14], (LAYERS, FF, D), FF ** -0.5, 0.0625, ((1, 2), (2, 16))),
    }


eps = 1e-06
theta_log = 13.815510557964274

def product(form, left, right):
    return jnp.einsum(form, left.astype(jnp.float32), right.astype(jnp.float32))

def rope_tables(position_ids, head_width):
    half_width = head_width // 2
    freq_index = jnp.arange(half_width).astype(jnp.float32)
    frequency = jnp.exp(-(2.0 * freq_index / head_width) * theta_log)
    angles = position_ids.astype(jnp.float32)[..., None] * frequency
    return (jnp.cos(angles), jnp.sin(angles))

def rotate(vectors, cosine, sine_table):
    half_width = vectors.shape[-1] // 2
    first_half = vectors[..., :half_width]
    second_half = vectors[..., half_width:]
    cos_wide = cosine[:, :, None, :]
    sin_wide = sine_table[:, :, None, :]
    return jnp.concatenate([first_half * cos_wide - second_half * sin_wide, second_half * cos_wide + first_half * sin_wide], axis=-1)

def unrotate(vectors, cosine, sine_table):
    half_width = vectors.shape[-1] // 2
    first_half = vectors[..., :half_width]
    second_half = vectors[..., half_width:]
    cos_wide = cosine[:, :, None, :]
    sin_wide = sine_table[:, :, None, :]
    return jnp.concatenate([first_half * cos_wide + second_half * sin_wide, second_half * cos_wide - first_half * sin_wide], axis=-1)

def norm_forward(stream, gain_vec):
    inv_scale = lax.rsqrt(lax.optimization_barrier(jnp.mean(stream * stream, axis=-1, keepdims=True)) + eps)
    unit_rows = stream * inv_scale
    return ((unit_rows * gain_vec.astype(jnp.float32)).astype(jnp.bfloat16), unit_rows, inv_scale)

def norm_backward(d_normed, unit_rows, inv_scale, gain_vec):
    d_unit = d_normed * gain_vec.astype(jnp.float32)
    d_gain = lax.optimization_barrier(jnp.sum(d_normed * unit_rows, axis=0))
    d_stream = inv_scale * (d_unit - unit_rows * lax.optimization_barrier(jnp.mean(d_unit * unit_rows, axis=-1, keepdims=True)))
    return (d_stream, d_gain)

def attend(queries, key_vecs, value_vecs, allowed, scale):
    scores = product('bqngd,bknd->bngqk', queries, key_vecs) * scale
    expo = jnp.exp(scores) * allowed[:, None, None]
    denom_sum = lax.optimization_barrier(jnp.sum(expo, axis=-1, keepdims=True))
    attention = (expo / denom_sum).astype(jnp.bfloat16)
    mixed = product('bngqk,bknd->bqngd', attention, value_vecs).astype(jnp.bfloat16)
    return (mixed, jnp.log(denom_sum))

def attend_backward(queries, key_vecs, value_vecs, allowed, log_total, d_mixed, scale):
    scores = product('bqngd,bknd->bngqk', queries, key_vecs) * scale
    probs_f = jnp.exp(scores - log_total) * allowed[:, None, None]
    d_value = product('bngqk,bqngd->bknd', probs_f.astype(jnp.bfloat16), d_mixed)
    d_probs = product('bqngd,bknd->bngqk', d_mixed, value_vecs)
    centre = lax.optimization_barrier(jnp.sum(probs_f * d_probs, axis=-1, keepdims=True))
    d_scores = (probs_f * (d_probs - centre) * scale).astype(jnp.bfloat16)
    d_query = product('bngqk,bknd->bqngd', d_scores, key_vecs)
    d_key = product('bngqk,bqngd->bknd', d_scores, queries)
    return (d_query, d_key, d_value)

def attn_forward(rows_in, weights, cosine, sine_table, allowed, sequences):
    w_query, w_key, w_value, w_out, b_query, b_key, b_value = weights[:7]
    head_count, head_width = b_query.shape
    group_count = b_key.shape[0]
    group_size = head_count // group_count
    row_count = rows_in.shape[0]
    span_length = row_count // sequences
    queries = jnp.dot(rows_in, w_query, preferred_element_type=jnp.float32) + b_query.reshape(-1).astype(jnp.float32)
    key_vecs = jnp.dot(rows_in, w_key, preferred_element_type=jnp.float32) + b_key.reshape(-1).astype(jnp.float32)
    value_vecs = (jnp.dot(rows_in, w_value, preferred_element_type=jnp.float32) + b_value.reshape(-1).astype(jnp.float32)).astype(jnp.bfloat16)
    queries = rotate(queries.reshape(sequences, span_length, head_count, head_width), cosine, sine_table).astype(jnp.bfloat16)
    queries = queries.reshape(sequences, span_length, group_count, group_size, head_width)
    key_vecs = rotate(key_vecs.reshape(sequences, span_length, group_count, head_width), cosine, sine_table).astype(jnp.bfloat16)
    value_vecs = value_vecs.reshape(sequences, span_length, group_count, head_width)
    mixed, log_total = attend(queries, key_vecs, value_vecs, allowed, head_width ** (-0.5))
    attn_rows = mixed.reshape(row_count, head_count * head_width)
    branch = jnp.dot(attn_rows, w_out, preferred_element_type=jnp.float32)
    return (branch, (queries, key_vecs, value_vecs, log_total, attn_rows))

def attn_backward(rows_in, weights, stored, d_out, cosine, sine_table, allowed, sequences):
    w_query, w_key, w_value, w_out, b_query, b_key, b_value = weights[:7]
    head_count, head_width = b_query.shape
    group_count = b_key.shape[0]
    queries, key_vecs, value_vecs, log_total, attn_rows = stored
    row_count = rows_in.shape[0]
    span_length = row_count // sequences
    d_o_weight = jnp.dot(attn_rows.T, d_out, preferred_element_type=jnp.float32)
    d_mixed = jnp.dot(d_out, w_out.T, preferred_element_type=jnp.float32).astype(jnp.bfloat16).reshape(queries.shape)
    d_query, d_key, d_value = attend_backward(queries, key_vecs, value_vecs, allowed, log_total, d_mixed, head_width ** (-0.5))
    d_query = unrotate(d_query.reshape(sequences, span_length, head_count, head_width), cosine, sine_table).reshape(row_count, -1)
    d_key = unrotate(d_key, cosine, sine_table).reshape(row_count, -1)
    d_value = d_value.reshape(row_count, -1)
    d_b_query = lax.optimization_barrier(jnp.sum(d_query, axis=0)).reshape(head_count, head_width)
    d_b_key = lax.optimization_barrier(jnp.sum(d_key, axis=0)).reshape(group_count, head_width)
    d_b_value = lax.optimization_barrier(jnp.sum(d_value, axis=0)).reshape(group_count, head_width)
    query_low = d_query.astype(jnp.bfloat16)
    key_low = d_key.astype(jnp.bfloat16)
    value_low = d_value.astype(jnp.bfloat16)
    d_rows = jnp.dot(query_low, w_query.T, preferred_element_type=jnp.float32)
    d_rows = d_rows + jnp.dot(key_low, w_key.T, preferred_element_type=jnp.float32)
    d_rows = d_rows + jnp.dot(value_low, w_value.T, preferred_element_type=jnp.float32)
    grads = (jnp.dot(rows_in.T, query_low, preferred_element_type=jnp.float32), jnp.dot(rows_in.T, key_low, preferred_element_type=jnp.float32), jnp.dot(rows_in.T, value_low, preferred_element_type=jnp.float32), d_o_weight, d_b_query, d_b_key, d_b_value)
    return (d_rows, grads)

def mlp_forward(rows_in, weights):
    w_gate, w_up, w_down = weights[:3]
    gate_pre = jnp.dot(rows_in, w_gate, preferred_element_type=jnp.float32)
    up_pre = jnp.dot(rows_in, w_up, preferred_element_type=jnp.float32)
    hidden_act = (jax.nn.silu(gate_pre) * up_pre).astype(jnp.bfloat16)
    return (jnp.dot(hidden_act, w_down, preferred_element_type=jnp.float32), (gate_pre, up_pre, hidden_act))

def mlp_backward(rows_in, weights, stored, d_out):
    w_gate, w_up, w_down = weights[:3]
    gate_pre, up_pre, hidden_act = stored
    d_down = jnp.dot(hidden_act.T, d_out, preferred_element_type=jnp.float32)
    d_hidden = jnp.dot(d_out, w_down.T, preferred_element_type=jnp.float32)
    sigmoid_g = jax.nn.sigmoid(gate_pre)
    d_gate = (d_hidden * up_pre * sigmoid_g * (1.0 + gate_pre * (1.0 - sigmoid_g))).astype(jnp.bfloat16)
    d_up = (d_hidden * gate_pre * sigmoid_g).astype(jnp.bfloat16)
    d_rows = jnp.dot(d_gate, w_gate.T, preferred_element_type=jnp.float32) + jnp.dot(d_up, w_up.T, preferred_element_type=jnp.float32)
    grads = (jnp.dot(rows_in.T, d_gate, preferred_element_type=jnp.float32), jnp.dot(rows_in.T, d_up, preferred_element_type=jnp.float32), d_down)
    return (d_rows, grads)

def reference(hidden_in, cotangent, segments, positions, norm_gains, q_weight, k_weight, v_weight, q_bias, k_bias, v_bias, o_weight, gate_weight, up_weight, down_weight):
    block_seqs = 16
    block_count = SEQS // block_seqs
    inputs_b = hidden_in.reshape(block_count, block_seqs, SEQ_LEN, D)
    cotan_b = cotangent.reshape(block_count, block_seqs, SEQ_LEN, D)
    segs_b = segments.reshape(block_count, block_seqs, SEQ_LEN)
    poss_b = positions.reshape(block_count, block_seqs, SEQ_LEN)
    places = jnp.arange(SEQ_LEN)
    causal = places[None, :] <= places[:, None]
    shapes = [norm_gains.shape, q_weight.shape, k_weight.shape, v_weight.shape, o_weight.shape, q_bias.shape, k_bias.shape, v_bias.shape, gate_weight.shape, up_weight.shape, down_weight.shape]
    start = tuple((jnp.zeros(shape_one, jnp.float32) for shape_one in shapes))

    def one_block(carry, item):
        block_in, block_dy, block_seg, block_pos = item
        cosine, sine_table = rope_tables(block_pos, HD)
        allowed = ((block_seg[:, :, None] == block_seg[:, None, :]) & causal[None]).astype(jnp.float32)
        stream = block_in.astype(jnp.float32).reshape(-1, D)
        kept = []
        for layer_no in range(LAYERS):
            attn_w = (q_weight[layer_no], k_weight[layer_no], v_weight[layer_no], o_weight[layer_no], q_bias[layer_no], k_bias[layer_no], v_bias[layer_no], norm_gains[layer_no, 0])
            mlp_w = (gate_weight[layer_no], up_weight[layer_no], down_weight[layer_no], norm_gains[layer_no, 1])
            normed_one, unit_one, inv_one = norm_forward(stream, attn_w[7])
            branch, stored_one = attn_forward(normed_one, attn_w, cosine, sine_table, allowed, block_seqs)
            mid_stream = stream + branch
            normed_two, unit_two, inv_two = norm_forward(mid_stream, mlp_w[3])
            branch, stored_two = mlp_forward(normed_two, mlp_w)
            stream = mid_stream + branch
            kept.append((attn_w, mlp_w, normed_one, unit_one, inv_one, stored_one, normed_two, unit_two, inv_two, stored_two))
        gradient = block_dy.reshape(-1, D)
        layer_grads = []
        for layer_no in reversed(range(LAYERS)):
            attn_w, mlp_w, normed_one, unit_one, inv_one, stored_one, normed_two, unit_two, inv_two, stored_two = kept[layer_no]
            d_rows, mlp_grads = mlp_backward(normed_two, mlp_w, stored_two, gradient.astype(jnp.bfloat16))
            d_norm, gain_two = norm_backward(d_rows, unit_two, inv_two, mlp_w[3])
            grad_mid = gradient + d_norm
            d_rows, attn_grads = attn_backward(normed_one, attn_w, stored_one, grad_mid.astype(jnp.bfloat16), cosine, sine_table, allowed, block_seqs)
            d_norm, gain_one = norm_backward(d_rows, unit_one, inv_one, attn_w[7])
            gradient = grad_mid + d_norm
            layer_grads.insert(0, (jnp.stack([gain_one, gain_two]),) + attn_grads + mlp_grads)
        stacked = tuple((jnp.stack([entry[index] for entry in layer_grads]) for index in range(11)))
        new_carry = tuple((old + new for old, new in zip(carry, stacked)))
        return (new_carry, (stream, gradient))
    totals, outputs = lax.scan(one_block, start, (inputs_b, cotan_b, segs_b, poss_b))
    hidden_out = outputs[0].reshape(TOKENS, D)
    input_grad = outputs[1].reshape(TOKENS, D)
    return (hidden_out, input_grad, totals[0], totals[1], totals[2], totals[3], totals[4], totals[5], totals[6], totals[7], totals[8], totals[9], totals[10])
```

```python
import jax
import jax.numpy as jnp
from jax import lax
from jax.sharding import Mesh
from jax.sharding import PartitionSpec as P

HD = 128
LAYERS = 1


eps = 1e-06
theta_log = 13.815510557964274


def product(form, left, right):
    return jnp.einsum(form, left, right, preferred_element_type=jnp.float32)


def rope_tables(position_ids, head_width):
    half_width = head_width // 2
    freq_index = jnp.arange(half_width).astype(jnp.float32)
    frequency = jnp.exp(-(2.0 * freq_index / head_width) * theta_log)
    angles = position_ids.astype(jnp.float32)[..., None] * frequency
    return (jnp.cos(angles), jnp.sin(angles))


def rotate(vectors, cosine, sine_table):
    half_width = vectors.shape[-1] // 2
    first_half = vectors[..., :half_width]
    second_half = vectors[..., half_width:]
    cos_wide = cosine[:, :, None, :]
    sin_wide = sine_table[:, :, None, :]
    return jnp.concatenate(
        [
            first_half * cos_wide - second_half * sin_wide,
            second_half * cos_wide + first_half * sin_wide,
        ],
        axis=-1,
    )


def unrotate(vectors, cosine, sine_table):
    half_width = vectors.shape[-1] // 2
    first_half = vectors[..., :half_width]
    second_half = vectors[..., half_width:]
    cos_wide = cosine[:, :, None, :]
    sin_wide = sine_table[:, :, None, :]
    return jnp.concatenate(
        [
            first_half * cos_wide + second_half * sin_wide,
            second_half * cos_wide - first_half * sin_wide,
        ],
        axis=-1,
    )


def norm_forward(stream, gain_vec):
    inv_scale = lax.rsqrt(jnp.mean(stream * stream, axis=-1, keepdims=True) + eps)
    unit_rows = stream * inv_scale
    return ((unit_rows * gain_vec.astype(jnp.float32)).astype(jnp.bfloat16), unit_rows, inv_scale)


def norm_backward(d_normed, unit_rows, inv_scale, gain_vec):
    d_unit = d_normed * gain_vec.astype(jnp.float32)
    d_gain = jnp.sum(d_normed * unit_rows, axis=0)
    d_stream = inv_scale * (
        d_unit - unit_rows * jnp.mean(d_unit * unit_rows, axis=-1, keepdims=True)
    )
    return (d_stream, d_gain)


def attend(queries, key_vecs, value_vecs, allowed, scale):
    scores = product("bqngd,bknd->bngqk", queries, key_vecs) * scale
    expo = jnp.exp(scores) * allowed[:, None, None]
    denom_sum = jnp.sum(expo, axis=-1, keepdims=True)
    attention = (expo / denom_sum).astype(jnp.bfloat16)
    mixed = product("bngqk,bknd->bqngd", attention, value_vecs).astype(jnp.bfloat16)
    return (mixed, jnp.log(denom_sum))


def attend_backward(queries, key_vecs, value_vecs, allowed, log_total, d_mixed, scale):
    scores = product("bqngd,bknd->bngqk", queries, key_vecs) * scale
    probs_f = jnp.exp(scores - log_total) * allowed[:, None, None]
    d_value = product("bngqk,bqngd->bknd", probs_f.astype(jnp.bfloat16), d_mixed)
    d_probs = product("bqngd,bknd->bngqk", d_mixed, value_vecs)
    centre = jnp.sum(probs_f * d_probs, axis=-1, keepdims=True)
    d_scores = (probs_f * (d_probs - centre) * scale).astype(jnp.bfloat16)
    d_query = product("bngqk,bknd->bqngd", d_scores, key_vecs)
    d_key = product("bngqk,bqngd->bknd", d_scores, queries)
    return (d_query, d_key, d_value)


def ring(size, step):
    return [(place, (place + step) % size) for place in range(size)]


def shift(values, axis_name, size, step):
    if step % size == 0:
        return values
    return lax.ppermute(values, axis_name, ring(size, step % size))


def ring_slots(values, axis_name, size):
    slots = [values]
    for _ in range(size - 1):
        slots.append(shift(slots[-1], axis_name, size, 1))
    return slots


def in_place_order(slots, own_index):
    size = len(slots)
    stacked = jnp.broadcast_to(slots[0][None], (size,) + slots[0].shape)
    for step in range(1, size):
        where = lax.rem(own_index - step + size, size)
        stacked = lax.dynamic_update_index_in_dim(stacked, slots[step], where, 0)
    return stacked


def pick(values, index, axis):
    return lax.dynamic_index_in_dim(values, index, axis, keepdims=False)


def make_step(z_size, r_size, c_size, t_size):
    def per_device(
        hidden_in,
        cotangent,
        segments,
        positions,
        norm_gains,
        q_weight,
        k_weight,
        v_weight,
        q_bias,
        k_bias,
        v_bias,
        o_weight,
        gate_weight,
        up_weight,
        down_weight,
    ):
        z_index = lax.axis_index("z")
        r_index = lax.axis_index("r")
        c_index = lax.axis_index("c")
        t_index = lax.axis_index("tensor")
        dp_size = z_size * r_size * c_size
        rows = q_weight.shape[1]
        width = rows * dp_size
        q_cols = q_weight.shape[2]
        kv_cols = k_weight.shape[2]
        heads = q_bias.shape[1]
        groups = k_bias.shape[1]
        group_size = heads // groups
        piece = q_bias.shape[2]
        hidden_units = gate_weight.shape[2]
        chunk = -(-hidden_units // (z_size * 128)) * 128
        own_tokens = hidden_in.shape[0]
        span = segments.shape[1]
        f32, bf16 = jnp.float32, jnp.bfloat16

        def gather_rows_of(block):
            z_slots = ring_slots(block, "z", z_size)
            z_blocks = []
            for slot in z_slots:
                r_blocks = in_place_order(ring_slots(slot, "r", r_size), r_index)
                z_blocks.append(in_place_order(ring_slots(r_blocks, "c", c_size), c_index))
            return in_place_order(z_blocks, z_index)

        small = jnp.concatenate(
            [
                norm_gains[0].reshape(-1),
                q_bias[0].reshape(-1),
                k_bias[0].reshape(-1),
                v_bias[0].reshape(-1),
            ]
        )
        qkv_cols = q_cols + 2 * kv_cols
        small_rows = jnp.pad(small[None], ((0, 7), (0, qkv_cols - small.shape[0])))
        qkv_block = jnp.concatenate(
            [jnp.concatenate([q_weight[0], k_weight[0], v_weight[0]], axis=1), small_rows], axis=0
        )
        qkv_all = gather_rows_of(qkv_block)
        small_all = qkv_all[:, :, :, rows, : small.shape[0]]
        small_all = small_all.transpose(0, 2, 1, 3).reshape(dp_size, small.shape[0])
        w_qkv = qkv_all[:, :, :, :rows].transpose(0, 2, 1, 3, 4).reshape(width, qkv_cols)
        gain_one = small_all[:, :rows].reshape(width)
        gain_two = small_all[:, rows : 2 * rows].reshape(width)
        at = 2 * rows
        b_query = small_all[:, at : at + heads * piece].reshape(dp_size, heads, piece)
        b_query = b_query.transpose(1, 0, 2).reshape(heads * HD)
        at = at + heads * piece
        b_key = small_all[:, at : at + groups * piece].reshape(dp_size, groups, piece)
        b_key = b_key.transpose(1, 0, 2).reshape(groups * HD)
        at = at + groups * piece
        b_value = small_all[:, at : at + groups * piece].reshape(dp_size, groups, piece)
        b_value = b_value.transpose(1, 0, 2).reshape(groups * HD)
        o_all = gather_rows_of(o_weight[0].T)
        w_out_t = o_all.transpose(0, 2, 1, 3, 4).reshape(width, q_cols)

        def chunked(weight):
            padded = jnp.pad(weight, ((0, 0), (0, z_size * chunk - hidden_units)))
            return padded.reshape(rows, z_size, chunk).transpose(1, 0, 2)

        ffn_block = jnp.concatenate(
            [chunked(gate_weight[0]), chunked(up_weight[0]), chunked(down_weight[0].T)], axis=2
        )
        z_blocks = []
        for step in range(z_size):
            target = lax.rem(z_index + step, z_size)
            slot = shift(pick(ffn_block, target, 0), "z", z_size, step)
            r_blocks = in_place_order(ring_slots(slot, "r", r_size), r_index)
            z_blocks.append(in_place_order(ring_slots(r_blocks, "c", c_size), c_index))
        ffn_all = in_place_order(z_blocks, z_index)
        ffn_all = ffn_all.transpose(0, 2, 1, 3, 4).reshape(width, 3 * chunk)
        w_gate_up = ffn_all[:, : 2 * chunk]
        w_down_t = ffn_all[:, 2 * chunk :]

        def gather_group_tokens(values):
            slots = ring_slots(values, "z", z_size)
            blocks = []
            for step in range(t_size):
                blocks.extend([shift(slot, "tensor", t_size, step) for slot in slots])
            return jnp.concatenate(blocks, axis=0)

        def scatter_group_tokens(partial):
            blocks = partial.reshape(t_size, z_size, own_tokens, width)
            total = None
            for z_step in range(z_size):
                summed = blocks[0, z_step]
                for t_step in range(1, t_size):
                    summed = summed + shift(
                        blocks[t_step, z_step].astype(bf16), "tensor", t_size, -t_step
                    ).astype(f32)
                if z_step:
                    summed = shift(summed.astype(bf16), "z", z_size, -z_step).astype(f32)
                total = summed if total is None else total + summed
            return total

        def pair_rows(values):
            return in_place_order(ring_slots(values, "tensor", t_size), t_index).reshape(
                t_size * values.shape[0], values.shape[1]
            )

        def pair_sum(partial):
            blocks = partial.reshape(t_size, own_tokens, width)
            total = pick(blocks, t_index, 0)
            for step in range(1, t_size):
                target = lax.rem(t_index + step, t_size)
                total = total + shift(
                    pick(blocks, target, 0).astype(bf16), "tensor", t_size, step
                ).astype(f32)
            return total

        grad_group = gather_group_tokens(cotangent.astype(bf16))

        cosine, sine_table = rope_tables(positions, HD)
        places = jnp.arange(span)
        causal = places[None, :] <= places[:, None]
        allowed = ((segments[:, :, None] == segments[:, None, :]) & causal[None]).astype(f32)
        scale = HD ** (-0.5)
        stream = hidden_in.astype(f32)
        normed_one, unit_one, inv_one = norm_forward(stream, gain_one)
        rows_one = pair_rows(normed_one)
        qkv = jnp.dot(rows_one, w_qkv, preferred_element_type=f32)
        queries = qkv[:, :q_cols] + b_query.astype(f32)
        keys = qkv[:, q_cols : q_cols + kv_cols] + b_key.astype(f32)
        values = (qkv[:, q_cols + kv_cols :] + b_value.astype(f32)).astype(bf16)
        queries = rotate(queries.reshape(1, span, heads, HD), cosine, sine_table).astype(bf16)
        queries = queries.reshape(1, span, groups, group_size, HD)
        keys = rotate(keys.reshape(1, span, groups, HD), cosine, sine_table).astype(bf16)
        values = values.reshape(1, span, groups, HD)
        mixed, log_total = attend(queries, keys, values, allowed, scale)
        attn_rows = mixed.reshape(span, heads * HD)
        branch = lax.dot_general(
            attn_rows, w_out_t, (((1,), (1,)), ((), ())), preferred_element_type=f32
        )
        mid = stream + pair_sum(branch)

        normed_two, unit_two, inv_two = norm_forward(mid, gain_two)
        rows_two = gather_group_tokens(normed_two)
        d_act = jnp.dot(grad_group, w_down_t, preferred_element_type=f32)
        gate_up = jnp.dot(rows_two, w_gate_up, preferred_element_type=f32)
        gate, up = gate_up[:, :chunk], gate_up[:, chunk:]
        sig = jax.nn.sigmoid(gate)
        act = (gate * sig * up).astype(bf16)
        d_gate = (d_act * up * sig * (1.0 + gate * (1.0 - sig))).astype(bf16)
        d_up = (d_act * gate * sig).astype(bf16)
        d_gate_up = jnp.concatenate([d_gate, d_up], axis=1)
        d_rows_two = lax.dot_general(
            d_gate_up, w_gate_up, (((1,), (1,)), ((), ())), preferred_element_type=f32
        )
        d_normed_two = scatter_group_tokens(d_rows_two)
        d_norm, gain_two_grad = norm_backward(d_normed_two, unit_two, inv_two, gain_two)
        grad_mid = cotangent + d_norm
        out_rows = lax.dot_general(
            act, w_down_t, (((1,), (1,)), ((), ())), preferred_element_type=f32
        )
        hidden_out = mid + scatter_group_tokens(out_rows)

        def row_product(left, right):
            return lax.dot_general(
                left, right, (((0,), (0,)), ((), ())), preferred_element_type=f32
            )

        def sum_over(blocks, axis, axis_name, size, own_index):
            total = pick(blocks, own_index, axis)
            for step in range(1, size):
                target = lax.rem(own_index + step, size)
                part = pick(blocks, target, axis).astype(bf16)
                total = total + shift(part, axis_name, size, step).astype(f32)
            return total

        def chip_rows(grad):
            blocks = grad.reshape(z_size, r_size, c_size, rows, grad.shape[1])
            blocks = sum_over(blocks, 2, "c", c_size, c_index)
            return sum_over(blocks, 1, "r", r_size, r_index)

        def ffn_rows(grad, count):
            blocks = chip_rows(grad)
            slots = []
            for step in range(z_size):
                target = lax.rem(z_index + step, z_size)
                part = pick(blocks, target, 0)
                if step:
                    part = shift(part.astype(bf16), "z", z_size, step).astype(f32)
                slots.append(part)
            whole = in_place_order(slots, z_index)
            whole = whole.reshape(z_size, rows, count, chunk).transpose(2, 1, 0, 3)
            return whole.reshape(count, rows, z_size * chunk)[:, :, :hidden_units]

        down_grad = ffn_rows(row_product(grad_group, act), 1)[0].T
        gate_grad, up_grad = ffn_rows(row_product(rows_two, d_gate_up), 2)

        rows_mid = pair_rows(grad_mid.astype(bf16))
        o_grad = row_product(rows_mid, attn_rows)
        d_mixed = jnp.dot(rows_mid, w_out_t, preferred_element_type=f32).astype(bf16)
        d_query, d_key, d_value = attend_backward(
            queries, keys, values, allowed, log_total, d_mixed.reshape(queries.shape), scale
        )
        d_query = unrotate(
            d_query.reshape(1, span, heads, HD), cosine, sine_table
        ).reshape(span, -1)
        d_key = unrotate(d_key, cosine, sine_table).reshape(span, -1)
        d_value = d_value.reshape(span, -1)
        q_bias_part = jnp.sum(d_query, axis=0).reshape(heads, dp_size, piece)
        k_bias_part = jnp.sum(d_key, axis=0)
        v_bias_part = jnp.sum(d_value, axis=0).reshape(groups, dp_size, piece)
        d_qkv = jnp.concatenate([d_query, d_key, d_value], axis=1).astype(bf16)
        d_rows_one = lax.dot_general(
            d_qkv, w_qkv, (((1,), (1,)), ((), ())), preferred_element_type=f32
        )
        d_norm, gain_one_grad = norm_backward(pair_sum(d_rows_one), unit_one, inv_one, gain_one)
        input_grad = grad_mid + d_norm
        qkv_grad = row_product(rows_one, d_qkv)

        def attn_rows_sum(grad):
            return sum_over(chip_rows(grad), 0, "z", z_size, z_index)

        o_grad = attn_rows_sum(o_grad).T
        qkv_grad = attn_rows_sum(qkv_grad)

        parts = jnp.concatenate(
            [
                q_bias_part.transpose(1, 0, 2).reshape(dp_size, heads * piece),
                v_bias_part.transpose(1, 0, 2).reshape(dp_size, groups * piece),
                jnp.broadcast_to(k_bias_part[None], (dp_size, groups * HD)),
                gain_one_grad.reshape(dp_size, rows),
                gain_two_grad.reshape(dp_size, rows),
            ],
            axis=1,
        ).reshape(z_size, r_size, c_size, -1)

        def sum_small(blocks, axis, axis_name, size, own_index):
            total = pick(blocks, own_index, axis)
            for step in range(1, size):
                target = lax.rem(own_index + step, size)
                total = total + shift(pick(blocks, target, axis), axis_name, size, step)
            return total

        parts = sum_small(parts, 2, "c", c_size, c_index)
        parts = sum_small(parts, 1, "r", r_size, r_index)
        parts = sum_small(parts, 0, "z", z_size, z_index)
        at = heads * piece
        q_bias_grad = parts[:at].reshape(heads, piece)
        v_bias_grad = parts[at : at + groups * piece].reshape(groups, piece)
        at = at + groups * piece
        k_bias_grad = parts[at : at + groups * HD].reshape(groups, HD)
        at = at + groups * HD
        gains = parts[at:].reshape(2, t_size, rows // t_size)
        gain_grads = sum_small(gains, 1, "tensor", t_size, t_index)
        return (
            hidden_out,
            input_grad,
            gain_grads[None],
            qkv_grad[None, :, :q_cols],
            qkv_grad[None, :, q_cols : q_cols + kv_cols],
            qkv_grad[None, :, q_cols + kv_cols :],
            o_grad[None],
            q_bias_grad[None],
            k_bias_grad[None],
            v_bias_grad[None],
            gate_grad[None],
            up_grad[None],
            down_grad[None],
        )

    return per_device


def solution(mesh):
    dp_size, t_size = mesh.shape["dp"], mesh.shape["tensor"]
    z_size, c_size = 4, 2
    r_size = dp_size // (z_size * c_size)
    fine = Mesh(
        mesh.devices.reshape(z_size, r_size, c_size, t_size), ("z", "r", "c", "tensor")
    )
    dp = ("z", "r", "c")
    every = ("z", "r", "c", "tensor")
    return jax.shard_map(
        make_step(z_size, r_size, c_size, t_size),
        mesh=fine,
        in_specs=(
            P(every, None),
            P(every, None),
            P(dp, None),
            P(dp, None),
            P(None, None, dp),
            P(None, dp, "tensor"),
            P(None, dp, "tensor"),
            P(None, dp, "tensor"),
            P(None, "tensor", dp),
            P(None, "tensor", dp),
            P(None, "tensor", dp),
            P(None, "tensor", dp),
            P(None, dp, "tensor"),
            P(None, dp, "tensor"),
            P(None, "tensor", dp),
        ),
        out_specs=(
            P(every, None),
            P(every, None),
            P(None, None, every),
            P(None, dp, "tensor"),
            P(None, dp, "tensor"),
            P(None, dp, "tensor"),
            P(None, "tensor", dp),
            P(None, "tensor", dp),
            P(None, "tensor", None),
            P(None, "tensor", dp),
            P(None, dp, "tensor"),
            P(None, dp, "tensor"),
            P(None, "tensor", dp),
        ),
        check_vma=False,
    )
```

```python
import functools

import jax
import jax.numpy as jnp
from jax import lax
from jax.sharding import Mesh
from jax.sharding import PartitionSpec as P
from jax.experimental import pallas as pl
from jax.experimental.pallas import tpu as pltpu


HD = 128


eps = 1e-06
theta_log = 13.815510557964274


def product(form, left, right):
    return jnp.einsum(form, left, right, preferred_element_type=jnp.float32)


def rope_tables(position_ids, head_width):
    half_width = head_width // 2
    freq_index = jnp.arange(half_width).astype(jnp.float32)
    frequency = jnp.exp(-(2.0 * freq_index / head_width) * theta_log)
    angles = position_ids.astype(jnp.float32)[..., None] * frequency
    return (jnp.cos(angles), jnp.sin(angles))


def rotate(vectors, cosine, sine_table):
    half_width = vectors.shape[-1] // 2
    first_half = vectors[..., :half_width]
    second_half = vectors[..., half_width:]
    cos_wide = cosine[:, :, None, :]
    sin_wide = sine_table[:, :, None, :]
    return jnp.concatenate(
        [
            first_half * cos_wide - second_half * sin_wide,
            second_half * cos_wide + first_half * sin_wide,
        ],
        axis=-1,
    )


def unrotate(vectors, cosine, sine_table):
    half_width = vectors.shape[-1] // 2
    first_half = vectors[..., :half_width]
    second_half = vectors[..., half_width:]
    cos_wide = cosine[:, :, None, :]
    sin_wide = sine_table[:, :, None, :]
    return jnp.concatenate(
        [
            first_half * cos_wide + second_half * sin_wide,
            second_half * cos_wide - first_half * sin_wide,
        ],
        axis=-1,
    )


def norm_forward(stream, gain_vec):
    inv_scale = lax.rsqrt(jnp.mean(stream * stream, axis=-1, keepdims=True) + eps)
    unit_rows = stream * inv_scale
    return ((unit_rows * gain_vec.astype(jnp.float32)).astype(jnp.bfloat16), unit_rows, inv_scale)


def norm_backward(d_normed, unit_rows, inv_scale, gain_vec):
    d_unit = d_normed * gain_vec.astype(jnp.float32)
    d_gain = jnp.sum(d_normed * unit_rows, axis=0)
    d_stream = inv_scale * (
        d_unit - unit_rows * jnp.mean(d_unit * unit_rows, axis=-1, keepdims=True)
    )
    return (d_stream, d_gain)


def attend(queries, key_vecs, value_vecs, allowed, scale):
    scores = product("bqngd,bknd->bngqk", queries, key_vecs) * scale
    expo = jnp.exp(scores) * allowed[:, None, None]
    denom_sum = jnp.sum(expo, axis=-1, keepdims=True)
    attention = (expo / denom_sum).astype(jnp.bfloat16)
    mixed = product("bngqk,bknd->bqngd", attention, value_vecs).astype(jnp.bfloat16)
    return (mixed, jnp.log(denom_sum))


def attend_backward(queries, key_vecs, value_vecs, allowed, log_total, d_mixed, scale):
    scores = product("bqngd,bknd->bngqk", queries, key_vecs) * scale
    probs_f = jnp.exp(scores - log_total) * allowed[:, None, None]
    d_value = product("bngqk,bqngd->bknd", probs_f.astype(jnp.bfloat16), d_mixed)
    d_probs = product("bqngd,bknd->bngqk", d_mixed, value_vecs)
    centre = jnp.sum(probs_f * d_probs, axis=-1, keepdims=True)
    d_scores = (probs_f * (d_probs - centre) * scale).astype(jnp.bfloat16)
    d_query = product("bngqk,bknd->bqngd", d_scores, key_vecs)
    d_key = product("bngqk,bqngd->bknd", d_scores, queries)
    return (d_query, d_key, d_value)


def ring(size, step):
    return [(place, (place + step) % size) for place in range(size)]


def shift(values, axis_name, size, step):
    if step % size == 0:
        return values
    return lax.ppermute(values, axis_name, ring(size, step % size))


def ring_slots(values, axis_name, size):
    slots = [values]
    for _ in range(1, size):
        slots.append(shift(slots[-1], axis_name, size, 1))
    return slots


def pick(values, index, axis):
    return lax.dynamic_index_in_dim(values, index, axis, keepdims=False)


def behind(axis_name, size, step):
    return lax.rem(lax.axis_index(axis_name) + (size - step), size)


def spec_any():
    return pl.BlockSpec(memory_space=pl.ANY)


def spec_vmem():
    return pl.BlockSpec(memory_space=pltpu.VMEM)


def gather_kernel(count, height, places, tail, *refs):
    pieces, refs = refs[:count], refs[count:]
    out_ref, refs = refs[0], refs[1:]
    tail_ref = None
    if tail:
        tail_ref, refs = refs[0], refs[1:]
    held, in_sems, out_sems, tail_sems = refs
    fetches = []
    tails = []
    for index in range(count):
        place = places(index)
        start = place * height if isinstance(place, int) else pl.multiple_of(place * height, 8)
        rows = pl.ds(start, height)
        fetch = pltpu.make_async_copy(
            pieces[index].at[pl.ds(0, height)], held.at[rows], in_sems.at[index]
        )
        fetch.start()
        fetches.append((fetch, rows))
        if tail:
            tail_rows = pl.ds(pl.multiple_of(place * 8, 8), 8)
            copy = pltpu.make_async_copy(
                pieces[index].at[pl.ds(height, 8), pl.ds(0, tail)],
                tail_ref.at[tail_rows],
                tail_sems.at[index],
            )
            copy.start()
            tails.append(copy)
    stores = []
    for index, (fetch, rows) in enumerate(fetches):
        fetch.wait()
        store = pltpu.make_async_copy(held.at[rows], out_ref.at[rows], out_sems.at[index])
        store.start()
        stores.append(store)
    for copy in stores + tails:
        copy.wait()


def gather_blocks(pieces, height, places, tail=0):
    count = len(pieces)
    cols = pieces[0].shape[1]
    dtype = pieces[0].dtype
    shapes = [jax.ShapeDtypeStruct((count * height, cols), dtype)]
    if tail:
        shapes.append(jax.ShapeDtypeStruct((count * 8, tail), dtype))
    held_bytes = count * height * cols * jnp.dtype(dtype).itemsize
    call = pl.pallas_call(
        functools.partial(gather_kernel, count, height, places, tail),
        out_shape=tuple(shapes),
        in_specs=[spec_any()] * count,
        out_specs=tuple(spec_any() for _ in shapes),
        scratch_shapes=[
            pltpu.VMEM((count * height, cols), dtype),
            pltpu.SemaphoreType.DMA((count,)),
            pltpu.SemaphoreType.DMA((count,)),
            pltpu.SemaphoreType.DMA((count,)),
        ],
        compiler_params=pltpu.CompilerParams(vmem_limit_bytes=held_bytes + (2 << 20)),
        cost_estimate=pl.CostEstimate(flops=0, bytes_accessed=2 * held_bytes, transcendentals=0),
    )
    out = call(*pieces)
    return out if tail else out[0]


def pack_kernel(z_size, chunk, *refs):
    weights, outs = refs[:3], refs[3:]
    hidden_units = weights[0].shape[1]
    last = hidden_units - (z_size - 1) * chunk
    for step in range(z_size):
        target = lax.rem(lax.axis_index("z") + step, z_size)
        for index, weight in enumerate(weights):
            columns = pl.ds(index * chunk, chunk)

            @pl.when(target < z_size - 1)
            def _():
                start = pl.multiple_of(target * chunk, 128)
                outs[step][:, columns] = weight[:, pl.ds(start, chunk)]

            @pl.when(target == z_size - 1)
            def _():
                outs[step][:, pl.ds(index * chunk, last)] = weight[:, hidden_units - last :]
                outs[step][:, pl.ds(index * chunk + last, chunk - last)] = jnp.zeros(
                    (weight.shape[0], chunk - last), weight.dtype
                )


def pack_chunks(weights, z_size, chunk):
    rows = weights[0].shape[0]
    block = jax.ShapeDtypeStruct((rows, 3 * chunk), weights[0].dtype)
    total = 2 * z_size * 3 * rows * chunk * 2
    return pl.pallas_call(
        functools.partial(pack_kernel, z_size, chunk),
        out_shape=(block,) * z_size,
        in_specs=[spec_vmem()] * 3,
        out_specs=(spec_vmem(),) * z_size,
        compiler_params=pltpu.CompilerParams(vmem_limit_bytes=total + (2 << 20)),
        cost_estimate=pl.CostEstimate(flops=0, bytes_accessed=total, transcendentals=0),
    )(*weights)


def spread_kernel(z_size, chunk, *refs):
    slots, outs = refs[:z_size], refs[z_size:]
    hidden_units = outs[0].shape[1]
    last = hidden_units - (z_size - 1) * chunk
    for step in range(z_size):
        source = behind("z", z_size, step)
        for index, out in enumerate(outs):

            @pl.when(source < z_size - 1)
            def _():
                start = pl.multiple_of(source * chunk, 128)
                out[:, pl.ds(start, chunk)] = slots[step][
                    :, pl.ds(index * chunk, chunk)
                ].astype(out.dtype)

            @pl.when(source == z_size - 1)
            def _():
                out[:, hidden_units - last :] = slots[step][
                    :, pl.ds(index * chunk, last)
                ].astype(out.dtype)


def spread_chunks(slots, count, hidden_units):
    z_size = len(slots)
    rows, cols = slots[0].shape
    total = rows * hidden_units * count * 8
    return pl.pallas_call(
        functools.partial(spread_kernel, z_size, cols // count),
        out_shape=(jax.ShapeDtypeStruct((rows, hidden_units), jnp.float32),) * count,
        in_specs=[spec_vmem()] * z_size,
        out_specs=(spec_vmem(),) * count,
        compiler_params=pltpu.CompilerParams(vmem_limit_bytes=total + (2 << 20)),
        cost_estimate=pl.CostEstimate(flops=0, bytes_accessed=total, transcendentals=0),
    )(*slots)


def make_step(z_size, r_size, c_size, t_size):
    def per_device(
        hidden_in,
        cotangent,
        segments,
        positions,
        norm_gains,
        q_weight,
        k_weight,
        v_weight,
        q_bias,
        k_bias,
        v_bias,
        o_weight,
        gate_weight,
        up_weight,
        down_weight,
    ):
        z_index = lax.axis_index("z")
        r_index = lax.axis_index("r")
        c_index = lax.axis_index("c")
        t_index = lax.axis_index("tensor")
        dp_size = z_size * r_size * c_size
        rows = q_weight.shape[1]
        width = rows * dp_size
        q_cols = q_weight.shape[2]
        kv_cols = k_weight.shape[2]
        heads = q_bias.shape[1]
        groups = k_bias.shape[1]
        group_size = heads // groups
        piece = q_bias.shape[2]
        hidden_units = gate_weight.shape[2]
        chunk = -(-hidden_units // (z_size * 128)) * 128
        own_tokens = hidden_in.shape[0]
        span = segments.shape[1]
        f32, bf16 = jnp.float32, jnp.bfloat16

        def row_places(index):
            z_step, rest = divmod(index, r_size * c_size)
            r_step, c_step = divmod(rest, c_size)
            place = behind("z", z_size, z_step) * r_size + behind("r", r_size, r_step)
            return place * c_size + behind("c", c_size, c_step)

        def chip_pieces(slots):
            pieces = []
            for slot in slots:
                r_slots = ring_slots(slot, "r", r_size)
                for r_slot in r_slots:
                    pieces.extend(ring_slots(r_slot, "c", c_size))
            return pieces

        small = jnp.concatenate(
            [
                norm_gains[0].reshape(-1),
                q_bias[0].reshape(-1),
                k_bias[0].reshape(-1),
                v_bias[0].reshape(-1),
            ]
        )
        qkv_cols = q_cols + 2 * kv_cols
        attn_cols = qkv_cols + q_cols
        small_rows = jnp.pad(small[None], ((0, 7), (0, attn_cols - small.shape[0])))
        attn_block = jnp.concatenate([q_weight[0], k_weight[0], v_weight[0], o_weight[0].T], axis=1)
        attn_block = jnp.concatenate([attn_block, small_rows], axis=0)
        w_attn, small_all = gather_blocks(
            chip_pieces(ring_slots(attn_block, "z", z_size)), rows, row_places, 256
        )
        w_qkv, w_out_t = w_attn[:, :qkv_cols], w_attn[:, qkv_cols:]
        small_all = small_all.reshape(dp_size, 8, 256)[:, 0]
        gain_one = small_all[:, :rows].reshape(width)
        gain_two = small_all[:, rows : 2 * rows].reshape(width)
        at = 2 * rows
        b_query = small_all[:, at : at + heads * piece].reshape(dp_size, heads, piece)
        b_query = b_query.transpose(1, 0, 2).reshape(heads * HD)
        at = at + heads * piece
        b_key = small_all[:, at : at + groups * piece].reshape(dp_size, groups, piece)
        b_key = b_key.transpose(1, 0, 2).reshape(groups * HD)
        at = at + groups * piece
        b_value = small_all[:, at : at + groups * piece].reshape(dp_size, groups, piece)
        b_value = b_value.transpose(1, 0, 2).reshape(groups * HD)
        blocks = pack_chunks((gate_weight[0], up_weight[0], down_weight[0].T), z_size, chunk)
        slots = [shift(block, "z", z_size, step) for step, block in enumerate(blocks)]
        ffn_all = gather_blocks(chip_pieces(slots), rows, row_places)
        w_gate_up = ffn_all[:, : 2 * chunk]
        w_down_t = ffn_all[:, 2 * chunk :]

        def gather_group_tokens(values):
            slots = ring_slots(values, "z", z_size)
            blocks = list(slots)
            for t_step in range(1, t_size):
                for slot in slots:
                    blocks.append(shift(slot, "tensor", t_size, t_step))
            return gather_blocks(blocks, own_tokens, int)

        def scatter_group_tokens(partial):
            blocks = partial.reshape(t_size, z_size, own_tokens, width)

            def over_tensor(z_step):
                total = blocks[0, z_step]
                for t_step in range(1, t_size):
                    part = blocks[t_step, z_step].astype(bf16)
                    part = shift(part, "tensor", t_size, -t_step)
                    total = total + part.astype(f32)
                return total

            total = over_tensor(1)
            for step in range(1, z_size):
                part = shift(total.astype(bf16), "z", z_size, 1)
                total = over_tensor((step + 1) % z_size) + part.astype(f32)
            return total

        def pair_rows(values):
            slots = ring_slots(values, "tensor", t_size)
            return gather_blocks(slots, own_tokens, lambda index: behind("tensor", t_size, index))

        def pair_sum(partial):
            blocks = partial.reshape(t_size, own_tokens, width)
            total = pick(blocks, t_index, 0)
            for step in range(1, t_size):
                target = lax.rem(t_index + step, t_size)
                part = pick(blocks, target, 0).astype(bf16)
                total = total + shift(part, "tensor", t_size, step).astype(f32)
            return total

        grad_group = gather_group_tokens(cotangent.astype(bf16))
        cosine, sine_table = rope_tables(positions, HD)
        places = jnp.arange(span)
        causal = places[None, :] <= places[:, None]
        allowed = ((segments[:, :, None] == segments[:, None, :]) & causal[None]).astype(f32)
        scale = HD ** (-0.5)
        stream = hidden_in.astype(f32)
        normed_one, unit_one, inv_one = norm_forward(stream, gain_one)
        rows_one = pair_rows(normed_one)
        qkv = jnp.dot(rows_one, w_qkv, preferred_element_type=f32)
        queries = qkv[:, :q_cols] + b_query.astype(f32)
        keys = qkv[:, q_cols : q_cols + kv_cols] + b_key.astype(f32)
        values = (qkv[:, q_cols + kv_cols :] + b_value.astype(f32)).astype(bf16)
        queries = rotate(queries.reshape(1, span, heads, HD), cosine, sine_table).astype(bf16)
        queries = queries.reshape(1, span, groups, group_size, HD)
        keys = rotate(keys.reshape(1, span, groups, HD), cosine, sine_table).astype(bf16)
        values = values.reshape(1, span, groups, HD)
        mixed, log_total = attend(queries, keys, values, allowed, scale)
        attn_rows = mixed.reshape(span, heads * HD)
        branch = lax.dot_general(
            attn_rows, w_out_t, (((1,), (1,)), ((), ())), preferred_element_type=f32
        )
        mid = stream + pair_sum(branch)

        normed_two, unit_two, inv_two = norm_forward(mid, gain_two)
        rows_two = gather_group_tokens(normed_two)
        d_act = jnp.dot(grad_group, w_down_t, preferred_element_type=f32)
        gate_up = jnp.dot(rows_two, w_gate_up, preferred_element_type=f32)
        gate, up = gate_up[:, :chunk], gate_up[:, chunk:]
        sig = jax.nn.sigmoid(gate)
        act = (gate * sig * up).astype(bf16)
        d_gate = (d_act * up * sig * (1.0 + gate * (1.0 - sig))).astype(bf16)
        d_up = (d_act * gate * sig).astype(bf16)
        d_gate_up = jnp.concatenate([d_gate, d_up], axis=1)
        d_rows_two = lax.dot_general(
            d_gate_up, w_gate_up, (((1,), (1,)), ((), ())), preferred_element_type=f32
        )
        d_normed_two = scatter_group_tokens(d_rows_two)
        d_norm, gain_two_grad = norm_backward(d_normed_two, unit_two, inv_two, gain_two)
        grad_mid = cotangent + d_norm
        out_rows = lax.dot_general(
            act, w_down_t, (((1,), (1,)), ((), ())), preferred_element_type=f32
        )
        hidden_out = mid + scatter_group_tokens(out_rows)

        def row_product(left, right):
            return lax.dot_general(
                left, right, (((0,), (0,)), ((), ())), preferred_element_type=f32
            )

        def sum_over(blocks, axis, axis_name, size, own_index):
            total = pick(blocks, own_index, axis)
            for step in range(1, size):
                target = lax.rem(own_index + step, size)
                part = pick(blocks, target, axis).astype(bf16)
                total = total + shift(part, axis_name, size, step).astype(f32)
            return total

        def chip_rows(grad):
            blocks = grad.reshape(z_size, r_size, c_size, rows, grad.shape[1])
            blocks = sum_over(blocks, 2, "c", c_size, c_index)
            return sum_over(blocks, 1, "r", r_size, r_index)

        def ffn_rows(grad, count):
            blocks = chip_rows(grad)
            slots = []
            for step in range(z_size):
                target = lax.rem(z_index + step, z_size)
                part = pick(blocks, target, 0)
                if step:
                    part = shift(part.astype(bf16), "z", z_size, step)
                slots.append(part)
            return spread_chunks(slots, count, hidden_units)

        down_grad = ffn_rows(row_product(grad_group, act), 1)[0].T
        gate_grad, up_grad = ffn_rows(row_product(rows_two, d_gate_up), 2)

        rows_mid = pair_rows(grad_mid.astype(bf16))
        o_grad = row_product(rows_mid, attn_rows)
        d_mixed = jnp.dot(rows_mid, w_out_t, preferred_element_type=f32).astype(bf16)
        d_query, d_key, d_value = attend_backward(
            queries, keys, values, allowed, log_total, d_mixed.reshape(queries.shape), scale
        )
        d_query = unrotate(
            d_query.reshape(1, span, heads, HD), cosine, sine_table
        ).reshape(span, -1)
        d_key = unrotate(d_key, cosine, sine_table).reshape(span, -1)
        d_value = d_value.reshape(span, -1)
        q_bias_part = jnp.sum(d_query, axis=0).reshape(heads, dp_size, piece)
        k_bias_part = jnp.sum(d_key, axis=0)
        v_bias_part = jnp.sum(d_value, axis=0).reshape(groups, dp_size, piece)
        d_qkv = jnp.concatenate([d_query, d_key, d_value], axis=1).astype(bf16)
        d_rows_one = lax.dot_general(
            d_qkv, w_qkv, (((1,), (1,)), ((), ())), preferred_element_type=f32
        )
        d_norm, gain_one_grad = norm_backward(pair_sum(d_rows_one), unit_one, inv_one, gain_one)
        input_grad = grad_mid + d_norm
        qkv_grad = row_product(rows_one, d_qkv)

        def attn_rows_sum(grad):
            return sum_over(chip_rows(grad), 0, "z", z_size, z_index)

        o_grad = attn_rows_sum(o_grad).T
        qkv_grad = attn_rows_sum(qkv_grad)

        parts = jnp.concatenate(
            [
                q_bias_part.transpose(1, 0, 2).reshape(dp_size, heads * piece),
                v_bias_part.transpose(1, 0, 2).reshape(dp_size, groups * piece),
                jnp.broadcast_to(k_bias_part[None], (dp_size, groups * HD)),
                gain_one_grad.reshape(dp_size, rows),
                gain_two_grad.reshape(dp_size, rows),
            ],
            axis=1,
        ).reshape(z_size, r_size, c_size, -1)

        def sum_small(blocks, axis, axis_name, size, own_index):
            total = pick(blocks, own_index, axis)
            for step in range(1, size):
                target = lax.rem(own_index + step, size)
                part = pick(blocks, target, axis)
                total = total + shift(part, axis_name, size, step)
            return total

        parts = sum_small(parts, 2, "c", c_size, c_index)
        parts = sum_small(parts, 1, "r", r_size, r_index)
        parts = sum_small(parts, 0, "z", z_size, z_index)
        at = heads * piece
        q_bias_grad = parts[:at].reshape(heads, piece)
        v_bias_grad = parts[at : at + groups * piece].reshape(groups, piece)
        at = at + groups * piece
        k_bias_grad = parts[at : at + groups * HD].reshape(groups, HD)
        at = at + groups * HD
        gains = parts[at:].reshape(2, t_size, rows // t_size)
        gain_grads = sum_small(gains, 1, "tensor", t_size, t_index)
        return (
            hidden_out,
            input_grad,
            gain_grads[None],
            qkv_grad[None, :, :q_cols],
            qkv_grad[None, :, q_cols : q_cols + kv_cols],
            qkv_grad[None, :, q_cols + kv_cols :],
            o_grad[None],
            q_bias_grad[None],
            k_bias_grad[None],
            v_bias_grad[None],
            gate_grad[None],
            up_grad[None],
            down_grad[None],
        )

    return per_device


def solution(mesh):
    dp_size, t_size = mesh.shape["dp"], mesh.shape["tensor"]
    z_size, c_size = 4, 2
    r_size = dp_size // (z_size * c_size)
    fine = Mesh(
        mesh.devices.reshape(z_size, r_size, c_size, t_size), ("z", "r", "c", "tensor")
    )
    dp = ("z", "r", "c")
    every = ("z", "r", "c", "tensor")
    inner = make_step(z_size, r_size, c_size, t_size)

    return jax.shard_map(
        inner,
        mesh=fine,
        in_specs=(
            P(every, None),
            P(every, None),
            P(dp, None),
            P(dp, None),
            P(None, None, dp),
            P(None, dp, "tensor"),
            P(None, dp, "tensor"),
            P(None, dp, "tensor"),
            P(None, "tensor", dp),
            P(None, "tensor", dp),
            P(None, "tensor", dp),
            P(None, "tensor", dp),
            P(None, dp, "tensor"),
            P(None, dp, "tensor"),
            P(None, "tensor", dp),
        ),
        out_specs=(
            P(every, None),
            P(every, None),
            P(None, None, every),
            P(None, dp, "tensor"),
            P(None, dp, "tensor"),
            P(None, dp, "tensor"),
            P(None, "tensor", dp),
            P(None, "tensor", dp),
            P(None, "tensor", None),
            P(None, "tensor", dp),
            P(None, dp, "tensor"),
            P(None, dp, "tensor"),
            P(None, "tensor", dp),
        ),
        check_vma=False,
    )
```

```python
import functools

import jax
import jax.numpy as jnp
from jax import lax
from jax.sharding import Mesh
from jax.sharding import PartitionSpec as P
from jax.experimental import pallas as pl
from jax.experimental.pallas import tpu as pltpu


HD = 128


eps = 1e-06
theta_log = 13.815510557964274


def rope_tables(position_ids, head_width):
    half_width = head_width // 2
    freq_index = jnp.arange(half_width).astype(jnp.float32)
    frequency = jnp.exp(-(2.0 * freq_index / head_width) * theta_log)
    angles = position_ids.astype(jnp.float32)[..., None] * frequency
    return (jnp.cos(angles), jnp.sin(angles))


def norm_forward(stream, gain_vec):
    inv_scale = lax.rsqrt(jnp.mean(stream * stream, axis=-1, keepdims=True) + eps)
    unit_rows = stream * inv_scale
    return ((unit_rows * gain_vec.astype(jnp.float32)).astype(jnp.bfloat16), unit_rows, inv_scale)


def norm_backward(d_normed, unit_rows, inv_scale, gain_vec):
    d_unit = d_normed * gain_vec.astype(jnp.float32)
    d_gain = jnp.sum(d_normed * unit_rows, axis=0)
    d_stream = inv_scale * (
        d_unit - unit_rows * jnp.mean(d_unit * unit_rows, axis=-1, keepdims=True)
    )
    return (d_stream, d_gain)


def ring(size, step):
    return [(place, (place + step) % size) for place in range(size)]


def shift(values, axis_name, size, step):
    if step % size == 0:
        return values
    return lax.ppermute(values, axis_name, ring(size, step % size))


def ring_slots(values, axis_name, size):
    slots = [values]
    for _ in range(1, size):
        slots.append(shift(slots[-1], axis_name, size, 1))
    return slots


def swap_z(values, step):
    return lax.ppermute(values, "z", [(place, place ^ step) for place in range(4)])


def z_slots(values):
    two = swap_z(values, 2)
    one = swap_z(values, 1)
    return [values, one, two, swap_z(two, 1)]


def z_sum(part, wire):
    dtype = part(0).dtype

    def moved(values, step):
        return swap_z(values.astype(wire), step).astype(dtype)

    two = part(2) + moved(part(3), 1)
    return part(0) + moved(part(1), 1) + moved(two, 2)


def pick(values, index, axis):
    return lax.dynamic_index_in_dim(values, index, axis, keepdims=False)


def across(step):
    return lax.bitwise_xor(lax.axis_index("z"), step)


def behind(axis_name, size, step):
    return lax.rem(lax.axis_index(axis_name) + (size - step), size)


def spec_any():
    return pl.BlockSpec(memory_space=pl.ANY)


def spec_vmem():
    return pl.BlockSpec(memory_space=pltpu.VMEM)


def pack_kernel(z_size, chunk, part, *refs):
    weights, outs = refs[:3], refs[3:]
    rows, hidden_units = weights[0].shape
    spare = z_size * chunk - hidden_units
    for step in range(z_size):
        target = across(step)
        start = target * chunk
        for index, weight in enumerate(weights):
            for first in range(0, chunk, part):
                out = outs[2 * step + index // 2]
                at = first if index == 2 else 2 * first + index * part
                is_last = first + part == chunk and spare > 0
                if not is_last:
                    out[:, pl.ds(at, part)] = weight[
                        :, pl.ds(pl.multiple_of(start + first, 128), part)
                    ]
                    continue

                @pl.when(target < z_size - 1)
                def _():
                    out[:, pl.ds(at, part)] = weight[
                        :, pl.ds(pl.multiple_of(start + first, 128), part)
                    ]

                @pl.when(target == z_size - 1)
                def _():
                    kept = part - spare
                    out[:, pl.ds(at, kept)] = weight[:, hidden_units - kept :]
                    out[:, pl.ds(at + kept, spare)] = jnp.zeros(
                        (rows, spare), weight.dtype
                    )


def pack_chunks(weights, z_size, chunk, part):
    rows = weights[0].shape[0]
    shapes = [
        jax.ShapeDtypeStruct((rows, count * chunk), weights[0].dtype) for count in (2, 1)
    ] * z_size
    total = 2 * z_size * 3 * rows * chunk * 2
    return pl.pallas_call(
        functools.partial(pack_kernel, z_size, chunk, part),
        out_shape=tuple(shapes),
        in_specs=[spec_vmem()] * 3,
        out_specs=tuple(spec_vmem() for _ in shapes),
        compiler_params=pltpu.CompilerParams(vmem_limit_bytes=total + (2 << 20)),
        cost_estimate=pl.CostEstimate(flops=0, bytes_accessed=total, transcendentals=0),
    )(*weights)


def spread_kernel(z_size, chunk, part, count, *refs):
    slots, outs = refs[:z_size], refs[z_size:]
    hidden_units = outs[0].shape[1]
    spare = z_size * chunk - hidden_units
    for step in range(z_size):
        source = across(step)
        start = source * chunk
        for index, out in enumerate(outs):
            for first in range(0, chunk, part):
                at = count * first + index * part
                is_last = first + part == chunk and spare > 0

                def move(kept):
                    block = slots[step][:, pl.ds(at, kept)].astype(out.dtype)
                    if kept == part:
                        out[:, pl.ds(pl.multiple_of(start + first, 128), part)] = block
                    else:
                        out[:, hidden_units - kept :] = block

                if not is_last:
                    move(part)
                    continue

                @pl.when(source < z_size - 1)
                def _():
                    move(part)

                @pl.when(source == z_size - 1)
                def _():
                    move(part - spare)


def spread_chunks(slots, count, part, hidden_units):
    z_size = len(slots)
    rows, cols = slots[0].shape
    total = rows * hidden_units * count * 8
    return pl.pallas_call(
        functools.partial(spread_kernel, z_size, cols // count, part, count),
        out_shape=(jax.ShapeDtypeStruct((rows, hidden_units), jnp.float32),) * count,
        in_specs=[spec_vmem()] * z_size,
        out_specs=(spec_vmem(),) * count,
        compiler_params=pltpu.CompilerParams(vmem_limit_bytes=total + (2 << 20)),
        cost_estimate=pl.CostEstimate(flops=0, bytes_accessed=total, transcendentals=0),
    )(*slots)


def attn_pack_kernel(gains, q_bias, k_bias, v_bias, q_w, k_w, v_w, o_w, out, sems):
    rows, _ = q_w.shape
    piece = q_bias.shape[1]
    copies = []
    at = 0
    for index, weight in enumerate((q_w, k_w, v_w, o_w)):
        cols = weight.shape[1]
        copy = pltpu.make_async_copy(
            weight, out.at[pl.ds(0, rows), pl.ds(at, cols)], sems.at[index]
        )
        copy.start()
        copies.append(copy)
        at += cols
    out[rows:, :] = jnp.zeros((16, out.shape[1]), out.dtype)
    out[rows : rows + 2, :rows] = gains[...]
    out[rows + 2 : rows + 8, :piece] = q_bias[...]
    out[rows + 8 : rows + 9, :piece] = k_bias[...]
    out[rows + 9 : rows + 10, :piece] = v_bias[...]
    for copy in copies:
        copy.wait()


def dot(left, right):
    return jnp.dot(left, right, preferred_element_type=jnp.float32)


def dot_nt(left, right):
    return lax.dot_general(
        left, right, (((1,), (1,)), ((), ())), preferred_element_type=jnp.float32
    )


def dot_tn(left, right):
    return lax.dot_general(
        left, right, (((0,), (0,)), ((), ())), preferred_element_type=jnp.float32
    )


def attn_fwd_kernel(heads, piece, places, *refs):
    own, other, cos_ref, sin_ref, allowed = refs[:5]
    pieces = refs[5:-15]
    (
        normed, q_out, k_out, v_out, p_out, rows_out, own_out, other_out, gains, w_out,
        branch, w_ref, tails, sems, w_sem,
    ) = refs[-15:]
    number = len(pieces)
    count, width = own.shape
    q_cols = heads * HD
    rows = width // number
    f32, bf16 = jnp.float32, jnp.bfloat16
    loads, ends = [], []
    for index, block in enumerate(pieces):
        start = pl.multiple_of(places(index) * rows, 8)
        end = pltpu.make_async_copy(
            block.at[pl.ds(rows, 16), pl.ds(0, width)], tails.at[index], sems.at[1, index]
        )
        end.start()
        ends.append(end)
        load = pltpu.make_async_copy(
            block.at[pl.ds(0, rows)], w_ref.at[pl.ds(start, rows)], sems.at[0, index]
        )
        load.start()
        loads.append(load)
    gain_sum = bias_sum = None
    for index, end in enumerate(ends):
        end.wait()
        gain = pltpu.roll(tails[index, :8, :].astype(f32), places(index) * rows, 1)
        bias = pltpu.roll(tails[index, :, :HD].astype(f32), places(index) * piece, 1)
        gain_sum = gain if gain_sum is None else gain_sum + gain
        bias_sum = bias if bias_sum is None else bias_sum + bias
    gains[...] = gain_sum
    place = lax.axis_index("tensor") * count
    for ref, start in ((own, place), (other, count - place)):
        block = ref[...].astype(f32)
        inv = lax.rsqrt(jnp.mean(block * block, axis=-1, keepdims=True) + eps)
        normed[pl.ds(pl.multiple_of(start, 128), count), :] = (
            block * inv * gain_sum[0:1, :]
        ).astype(bf16)
    for load in loads:
        load.wait()
    keep = pltpu.make_async_copy(w_ref, w_out, w_sem)
    keep.start()
    qkv = dot(normed[...], w_ref[:, : q_cols + 2 * HD])
    cosine, sine = cos_ref[...], sin_ref[...]

    def turn(values):
        return (values * cosine + pltpu.roll(values, HD // 2, 1) * sine).astype(bf16)

    keys = turn(qkv[:, q_cols : q_cols + HD] + bias_sum[8:9, :])
    values = (qkv[:, q_cols + HD :] + bias_sum[9:10, :]).astype(bf16)
    k_out[...] = keys
    v_out[...] = values
    for head in range(heads):
        columns = pl.ds(head * HD, HD)
        query = turn(qkv[:, head * HD : (head + 1) * HD] + bias_sum[2 + head : 3 + head, :])
        q_out[:, columns] = query
        expo = jnp.exp(dot_nt(query, keys) * HD ** (-0.5)) * allowed[...]
        probs = expo / jnp.sum(expo, axis=-1, keepdims=True)
        p_out[head] = probs
        rows_out[:, columns] = dot(probs.astype(bf16), values).astype(bf16)
    branch[...] = dot_nt(rows_out[...], w_ref[:, q_cols + 2 * HD :])
    own_out[...] = branch[pl.ds(pl.multiple_of(place, 128), count), :]
    other_out[...] = branch[pl.ds(pl.multiple_of(count - place, 128), count), :].astype(bf16)
    keep.wait()


def attn_forward(own, other, cosine, sine, allowed, pieces, places, heads, piece, t_size):
    count, width = own.shape
    span = count * t_size
    q_cols = heads * HD
    cols = pieces[0].shape[1]
    number = len(pieces)
    f32, bf16 = jnp.float32, jnp.bfloat16
    shapes = (
        ((span, width), bf16),
        ((span, q_cols), bf16),
        ((span, HD), bf16),
        ((span, HD), bf16),
        ((heads, span, span), f32),
        ((span, q_cols), bf16),
        ((count, width), f32),
        ((count, width), bf16),
        ((8, width), f32),
        ((width, cols), bf16),
    )
    return pl.pallas_call(
        functools.partial(attn_fwd_kernel, heads, piece, places),
        out_shape=tuple(jax.ShapeDtypeStruct(*shape) for shape in shapes),
        in_specs=[spec_vmem()] * 5 + [spec_any()] * number,
        out_specs=tuple(spec_vmem() for _ in shapes[:-1]) + (spec_any(),),
        scratch_shapes=[
            pltpu.VMEM((span, width), f32),
            pltpu.VMEM((width, cols), bf16),
            pltpu.VMEM((number, 16, width), bf16),
            pltpu.SemaphoreType.DMA((2, number)),
            pltpu.SemaphoreType.DMA(()),
        ],
        compiler_params=pltpu.CompilerParams(vmem_limit_bytes=40 << 20),
        cost_estimate=pl.CostEstimate(
            flops=2 * span * width * (q_cols * 2 + 2 * HD), bytes_accessed=12 << 20,
            transcendentals=heads * span * span,
        ),
    )(own, other, cosine, sine, allowed, *pieces)


def attn_bwd_kernel(
    heads, own, other, w_ref, q_ref, k_ref, v_ref, p_ref, cos_ref, sin_ref,
    rows_mid, d_qkv, sums, own_out, other_out, d_attn, d_rows,
):
    count, _ = own.shape
    q_cols = heads * HD
    bf16 = jnp.bfloat16
    place = lax.axis_index("tensor") * count
    rows_mid[pl.ds(pl.multiple_of(place, 128), count), :] = own[...]
    rows_mid[pl.ds(pl.multiple_of(count - place, 128), count), :] = other[...]
    d_attn[...] = dot(rows_mid[...], w_ref[:, q_cols + 2 * HD :]).astype(bf16)
    cosine, sine = cos_ref[...], sin_ref[...]
    keys, values = k_ref[...], v_ref[...]

    def turn_back(grad, columns):
        turned = grad * cosine - pltpu.roll(grad, HD // 2, 1) * sine
        sums[:, columns] = jnp.sum(turned, axis=0, keepdims=True)
        d_qkv[:, columns] = turned.astype(bf16)

    d_key = d_value = None
    for head in range(heads):
        columns = pl.ds(head * HD, HD)
        d_head = d_attn[:, columns]
        probs = p_ref[head]
        d_value_part = dot_tn(probs.astype(bf16), d_head)
        d_probs = dot_nt(d_head, values)
        centre = jnp.sum(probs * d_probs, axis=-1, keepdims=True)
        d_scores = (probs * (d_probs - centre) * HD ** (-0.5)).astype(bf16)
        turn_back(dot(d_scores, keys), columns)
        d_key_part = dot_tn(d_scores, q_ref[:, columns])
        d_key = d_key_part if d_key is None else d_key + d_key_part
        d_value = d_value_part if d_value is None else d_value + d_value_part
    turn_back(d_key, pl.ds(q_cols, HD))
    sums[:, q_cols + HD :] = jnp.sum(d_value, axis=0, keepdims=True)
    d_qkv[:, q_cols + HD :] = d_value.astype(bf16)
    d_rows[...] = dot_nt(d_qkv[...], w_ref[:, : q_cols + 2 * HD])
    own_out[...] = d_rows[pl.ds(pl.multiple_of(place, 128), count), :]
    other_out[...] = d_rows[pl.ds(pl.multiple_of(count - place, 128), count), :].astype(bf16)


def attn_backward(own, other, w_attn, q, k, v, probs, cosine, sine, heads, t_size):
    count, width = own.shape
    span = count * t_size
    q_cols = heads * HD
    f32, bf16 = jnp.float32, jnp.bfloat16
    shapes = (
        ((span, width), bf16),
        ((span, q_cols + 2 * HD), bf16),
        ((1, q_cols + 2 * HD), f32),
        ((count, width), f32),
        ((count, width), bf16),
    )
    return pl.pallas_call(
        functools.partial(attn_bwd_kernel, heads),
        out_shape=tuple(jax.ShapeDtypeStruct(*shape) for shape in shapes),
        in_specs=[spec_vmem()] * 9,
        out_specs=tuple(spec_vmem() for _ in shapes),
        scratch_shapes=[pltpu.VMEM((span, q_cols), bf16), pltpu.VMEM((span, width), f32)],
        compiler_params=pltpu.CompilerParams(vmem_limit_bytes=40 << 20),
        cost_estimate=pl.CostEstimate(
            flops=2 * span * width * (q_cols * 2 + 2 * HD), bytes_accessed=12 << 20,
            transcendentals=0,
        ),
    )(own, other, w_attn, q, k, v, probs, cosine, sine)


def piece_load(pieces, index, places, step, cols, w, sems):
    rows = pieces[index].shape[0]
    start = pl.multiple_of(places(index) * rows, 8)
    at = step * cols if isinstance(step, int) else pl.multiple_of(step * cols, 128)
    return pltpu.make_async_copy(
        pieces[index].at[:, pl.ds(at, cols)], w.at[step, pl.ds(start, rows)], sems.at[step, index]
    )


def turn_store(w, w_out, step, sems):
    cols = w.shape[2]
    at = step * cols if isinstance(step, int) else pl.multiple_of(step * cols, 128)
    return pltpu.make_async_copy(w.at[step], w_out.at[:, pl.ds(at, cols)], sems.at[step])


def token_load(blocks, index, held, sems):
    height = blocks[index].shape[0]
    return pltpu.make_async_copy(
        blocks[index], held.at[pl.ds(index * height, height)], sems.at[index]
    )


def ffn_fwd_kernel(count, part, places, *refs):
    x_refs, refs = refs[:count], refs[count:]
    pieces, refs = refs[:-10], refs[-10:]
    act_out, slope_out, w_out, x_out, x_all, w, loads, stores, x_loads, x_store = refs
    bf16 = jnp.bfloat16
    step = pl.program_id(0)
    turns = w.shape[0]
    keep_x = pltpu.make_async_copy(x_all, x_out, x_store)

    @pl.when(step == 0)
    def _():
        for index in range(count):
            token_load(x_refs, index, x_all, x_loads).start()
        for turn in range(turns):
            for index in range(len(pieces)):
                piece_load(pieces, index, places, turn, 2 * part, w, loads).start()
        for index in range(count):
            token_load(x_refs, index, x_all, x_loads).wait()
        keep_x.start()

    for index in range(len(pieces)):
        piece_load(pieces, index, places, step, 2 * part, w, loads).wait()
    turn_store(w, w_out, step, stores).start()
    height = x_all.shape[0] // 4
    for block in range(4):
        rows = pl.ds(block * height, height)
        gate_up = dot(x_all[rows, :], w[step])
        gate, up = gate_up[:, :part], gate_up[:, part:]
        sig = 0.5 * jnp.tanh(0.5 * gate) + 0.5
        swish = gate * sig
        act_out[rows, :] = (swish * up).astype(bf16)
        slope_out[rows, :part] = (up * (sig + swish * (1.0 - sig))).astype(bf16)
        slope_out[rows, part:] = swish.astype(bf16)

    @pl.when(step == turns - 1)
    def _():
        for turn in range(turns):
            turn_store(w, w_out, turn, stores).wait()
        keep_x.wait()


def ffn_forward(x_blocks, pieces, places, part):
    count = len(x_blocks)
    height, width = x_blocks[0].shape
    tokens = count * height
    chunk = pieces[0].shape[1] // 2
    turns = chunk // part
    bf16 = jnp.bfloat16
    return pl.pallas_call(
        functools.partial(ffn_fwd_kernel, count, part, places),
        grid=(turns,),
        out_shape=(
            jax.ShapeDtypeStruct((tokens, chunk), bf16),
            jax.ShapeDtypeStruct((tokens, 2 * chunk), bf16),
            jax.ShapeDtypeStruct((width, 2 * chunk), bf16),
            jax.ShapeDtypeStruct((tokens, width), bf16),
        ),
        in_specs=[spec_any()] * (count + len(pieces)),
        out_specs=(
            pl.BlockSpec((tokens, part), lambda j: (0, j)),
            pl.BlockSpec((tokens, 2 * part), lambda j: (0, j)),
            spec_any(),
            spec_any(),
        ),
        scratch_shapes=[
            pltpu.VMEM((tokens, width), bf16),
            pltpu.VMEM((turns, width, 2 * part), bf16),
            pltpu.SemaphoreType.DMA((turns, len(pieces))),
            pltpu.SemaphoreType.DMA((turns,)),
            pltpu.SemaphoreType.DMA((count,)),
            pltpu.SemaphoreType.DMA(()),
        ],
        compiler_params=pltpu.CompilerParams(vmem_limit_bytes=36 << 20),
        cost_estimate=pl.CostEstimate(
            flops=4 * tokens * width * chunk, bytes_accessed=30 << 20,
            transcendentals=tokens * chunk,
        ),
    )(*x_blocks, *pieces)


def ffn_bwd_kernel(count, number, part, half, places, *refs):
    g_refs, refs = refs[:count], refs[count:]
    pieces, refs = refs[:number], refs[number:]
    w_gu, slope, refs = refs[0], refs[1], refs[2:]
    if number:
        d_out, rows_out, g_out, w_out, g_all, total, g_loads, g_store, w, loads, stores = refs
    else:
        w_d, _, _, d_out, rows_out, g_out, g_all, total, g_loads, g_store = refs
    bf16, f32 = jnp.bfloat16, jnp.float32
    step = pl.program_id(0)
    turns = pl.num_programs(0)
    tokens = g_all.shape[0]
    keep_g = pltpu.make_async_copy(g_all, g_out.at[pl.ds(half * tokens, tokens)], g_store)

    @pl.when(step == 0)
    def _():
        for index in range(count):
            token_load(g_refs, index, g_all, g_loads).start()
        if number:
            for turn in range(w.shape[0]):
                for index in range(number):
                    piece_load(pieces, index, places, turn, part, w, loads).start()
        for index in range(count):
            token_load(g_refs, index, g_all, g_loads).wait()
        keep_g.start()

    if number:
        for index in range(number):
            piece_load(pieces, index, places, step, part, w, loads).wait()
        turn_store(w, w_out, step, stores).start()
    height = tokens // 2
    for block in range(2):
        span = pl.ds(block * height, height)
        d_act = dot(g_all[span, :], w[step] if number else w_d[...])
        d_out[span, :part] = (d_act * slope[span, :part].astype(f32)).astype(bf16)
        d_out[span, part:] = (d_act * slope[span, part:].astype(f32)).astype(bf16)
        rows = dot_nt(d_out[span, :], w_gu[...])

        @pl.when(step == 0)
        def _():
            total[span, :] = rows

        @pl.when(jnp.logical_and(step > 0, step < turns - 1))
        def _():
            total[span, :] += rows

        @pl.when(step == turns - 1)
        def _():
            rows_out[span, :] = (total[span, :] + rows).astype(rows_out.dtype)

    @pl.when(step == turns - 1)
    def _():
        if number:
            for turn in range(w.shape[0]):
                turn_store(w, w_out, turn, stores).wait()
        keep_g.wait()


def ffn_backward(half, g_blocks, w_gu, slope, part, dtype, pieces, places, held=()):
    count, number = len(g_blocks), len(pieces)
    height, width = g_blocks[0].shape
    tokens = count * height
    chunk = w_gu.shape[1] // 2
    turns = chunk // part
    bf16 = jnp.bfloat16
    d_spec = pl.BlockSpec((tokens, 2 * part), lambda j: (half, j))
    shapes = [
        jax.ShapeDtypeStruct((2 * tokens, 2 * chunk), bf16),
        jax.ShapeDtypeStruct((tokens, width), dtype),
        jax.ShapeDtypeStruct((2 * tokens, width), bf16),
    ]
    out_specs = [d_spec, pl.BlockSpec((tokens, width), lambda j: (0, 0)), spec_any()]
    in_specs = [spec_any()] * (count + number) + [
        pl.BlockSpec((width, 2 * part), lambda j: (0, j)),
        d_spec,
    ]
    scratch = [
        pltpu.VMEM((tokens, width), bf16),
        pltpu.VMEM((tokens, width), jnp.float32),
        pltpu.SemaphoreType.DMA((count,)),
        pltpu.SemaphoreType.DMA(()),
    ]
    aliases = {}
    if number:
        shapes.append(jax.ShapeDtypeStruct((width, chunk), bf16))
        out_specs.append(spec_any())
        scratch += [
            pltpu.VMEM((turns, width, part), bf16),
            pltpu.SemaphoreType.DMA((turns, number)),
            pltpu.SemaphoreType.DMA((turns,)),
        ]
    else:
        in_specs += [pl.BlockSpec((width, part), lambda j: (0, j)), spec_any(), spec_any()]
        aliases = {count + 3: 0, count + 4: 2}
    return pl.pallas_call(
        functools.partial(ffn_bwd_kernel, count, number, part, half, places),
        grid=(turns,),
        out_shape=tuple(shapes),
        in_specs=in_specs,
        out_specs=tuple(out_specs),
        scratch_shapes=scratch,
        input_output_aliases=aliases,
        compiler_params=pltpu.CompilerParams(vmem_limit_bytes=36 << 20),
        cost_estimate=pl.CostEstimate(
            flops=6 * tokens * width * chunk, bytes_accessed=20 << 20, transcendentals=0
        ),
    )(*g_blocks, *pieces, w_gu, slope, *held)


def make_step(z_size, r_size, c_size, t_size):
    def per_device(
        hidden_in,
        cotangent,
        segments,
        positions,
        norm_gains,
        q_weight,
        k_weight,
        v_weight,
        q_bias,
        k_bias,
        v_bias,
        o_weight,
        gate_weight,
        up_weight,
        down_weight,
    ):
        r_index = lax.axis_index("r")
        c_index = lax.axis_index("c")
        t_index = lax.axis_index("tensor")
        dp_size = z_size * r_size * c_size
        rows = q_weight.shape[1]
        width = rows * dp_size
        q_cols = q_weight.shape[2]
        kv_cols = k_weight.shape[2]
        heads = q_bias.shape[1]
        groups = k_bias.shape[1]
        piece = q_bias.shape[2]
        hidden_units = gate_weight.shape[2]
        chunk = -(-hidden_units // (z_size * 384)) * 384
        turn = 384
        own_tokens = hidden_in.shape[0]
        span = segments.shape[1]
        f32, bf16 = jnp.float32, jnp.bfloat16

        def row_places(index):
            z_step, rest = divmod(index, r_size * c_size)
            r_step, c_step = divmod(rest, c_size)
            place = across(z_step) * r_size + behind("r", r_size, r_step)
            return place * c_size + behind("c", c_size, c_step)

        def chip_pieces(slots):
            pieces = []
            for slot in slots:
                r_slots = ring_slots(slot, "r", r_size)
                for r_slot in r_slots:
                    pieces.extend(ring_slots(r_slot, "c", c_size))
            return pieces

        def gather_group_tokens(values):
            slots = z_slots(values)
            blocks = list(slots)
            for t_step in range(1, t_size):
                for slot in slots:
                    blocks.append(shift(slot, "tensor", t_size, t_step))
            return blocks

        attn_cols = 2 * q_cols + 2 * kv_cols
        call = pl.pallas_call(
            attn_pack_kernel,
            out_shape=jax.ShapeDtypeStruct((rows + 16, attn_cols), bf16),
            in_specs=[spec_vmem()] * 4 + [spec_any()] * 4,
            out_specs=spec_vmem(),
            scratch_shapes=[pltpu.SemaphoreType.DMA((4,))],
            compiler_params=pltpu.CompilerParams(vmem_limit_bytes=4 << 20),
        )
        attn_block = call(
            norm_gains[0], q_bias[0], k_bias[0], v_bias[0],
            q_weight[0], k_weight[0], v_weight[0], o_weight[0].T,
        )
        a_pieces = chip_pieces(z_slots(attn_block))

        blocks = pack_chunks((gate_weight[0], up_weight[0], down_weight[0].T), z_size, chunk, turn)

        def weight_pieces(blocks):
            slots = [swap_z(block, step) if step else block for step, block in enumerate(blocks)]
            return chip_pieces(slots)

        e_pieces = weight_pieces(blocks[0::2])
        f_pieces = weight_pieces(blocks[1::2])

        def scatter_group_tokens(kept, sent):
            kept = kept.reshape(z_size, own_tokens, width)
            sent = sent.reshape(z_size, own_tokens, width)

            def over_tensor(z_step):
                part = shift(sent[z_step], "tensor", t_size, 1)
                return kept[z_step] + part.astype(f32)

            return z_sum(over_tensor, bf16)

        def swap_rows(values):
            return shift(values, "tensor", t_size, 1)

        g_blocks = gather_group_tokens(cotangent.astype(bf16))

        half_cos, half_sin = rope_tables(positions[0], HD)
        cosine = jnp.concatenate([half_cos, half_cos], axis=1)
        sine = jnp.concatenate([-half_sin, half_sin], axis=1)
        places = jnp.arange(span)
        causal = places[None, :] <= places[:, None]
        allowed = ((segments[0][:, None] == segments[0][None, :]) & causal).astype(f32)
        stream = hidden_in.astype(f32)
        rows_one, q, k, v, probs, attn_rows, kept, sent, gains, w_attn = attn_forward(
            hidden_in, swap_rows(hidden_in), cosine, sine, allowed, a_pieces, row_places,
            heads, piece, t_size,
        )
        gain_one, gain_two = gains[0], gains[1]
        mid = stream + kept + swap_rows(sent).astype(f32)

        normed_two, unit_two, inv_two = norm_forward(mid, gain_two)
        n_blocks = gather_group_tokens(normed_two)
        half = len(n_blocks) // 2
        act, slope, w_gate_up, rows_two = ffn_forward(n_blocks, e_pieces, row_places, turn)
        d_gate_up, d_sent, grad_group, w_down_t = ffn_backward(
            1, g_blocks[half:], w_gate_up, slope, turn, bf16, f_pieces, row_places
        )
        d_gate_up, d_kept, grad_group = ffn_backward(
            0, g_blocks[:half], w_gate_up, slope, turn, f32, (), row_places,
            (w_down_t, d_gate_up, grad_group),
        )
        d_normed_two = scatter_group_tokens(d_kept, d_sent)
        d_norm, gain_two_grad = norm_backward(d_normed_two, unit_two, inv_two, gain_two)
        grad_mid = cotangent + d_norm
        tokens = act.shape[0] // 2
        out_sent = dot_nt(act[tokens:], w_down_t).astype(bf16)
        out_kept = dot_nt(act[:tokens], w_down_t)
        out_total = scatter_group_tokens(out_kept, out_sent)

        def sum_over(blocks, axis, axis_name, size, own_index):
            total = pick(blocks, own_index, axis)
            for step in range(1, size):
                target = lax.rem(own_index + step, size)
                part = pick(blocks, target, axis).astype(bf16)
                total = total + shift(part, axis_name, size, step).astype(f32)
            return total

        def chip_rows(grad):
            blocks = grad.reshape(z_size, r_size, c_size, rows, grad.shape[1])
            blocks = sum_over(blocks, 2, "c", c_size, c_index)
            return sum_over(blocks, 1, "r", r_size, r_index)

        def ffn_rows(grad, count):
            blocks = chip_rows(grad)
            slots = []
            for step in range(z_size):
                part = pick(blocks, across(step), 0)
                if step:
                    part = swap_z(part.astype(bf16), step)
                slots.append(part)
            return spread_chunks(slots, count, turn, hidden_units)

        grad_gate_up = dot_tn(rows_two, d_gate_up)
        grad_down = dot_tn(grad_group, act)
        gate_grad, up_grad = ffn_rows(grad_gate_up, 2)
        down_grad = ffn_rows(grad_down, 1)[0].T

        mid_low = grad_mid.astype(bf16)
        rows_mid, d_qkv, sums, kept, sent = attn_backward(
            mid_low, swap_rows(mid_low), w_attn, q, k, v, probs, cosine, sine, heads, t_size
        )
        out_total, kept = lax.optimization_barrier((out_total, kept))
        hidden_out = mid + out_total
        d_normed_one = kept + swap_rows(sent).astype(f32)
        _, unit_one, inv_one = norm_forward(stream, gain_one)
        d_norm, gain_one_grad = norm_backward(d_normed_one, unit_one, inv_one, gain_one)
        input_grad = grad_mid + d_norm
        o_grad = dot_tn(rows_mid, attn_rows)
        qkv_grad = dot_tn(rows_one, d_qkv)
        q_bias_part = sums[0, :q_cols].reshape(heads, dp_size, piece)
        k_bias_part = sums[0, q_cols : q_cols + kv_cols]
        v_bias_part = sums[0, q_cols + kv_cols :].reshape(groups, dp_size, piece)

        def attn_rows_sum(grad):
            blocks = chip_rows(grad)
            return z_sum(lambda step: pick(blocks, across(step), 0), bf16)

        o_grad = attn_rows_sum(o_grad).T
        qkv_grad = attn_rows_sum(qkv_grad)

        parts = jnp.concatenate(
            [
                q_bias_part.transpose(1, 0, 2).reshape(dp_size, heads * piece),
                v_bias_part.transpose(1, 0, 2).reshape(dp_size, groups * piece),
                jnp.broadcast_to(k_bias_part[None], (dp_size, groups * HD)),
                gain_one_grad.reshape(dp_size, rows),
                gain_two_grad.reshape(dp_size, rows),
            ],
            axis=1,
        ).reshape(z_size, r_size, c_size, -1)

        def sum_small(blocks, axis, axis_name, size, own_index):
            total = pick(blocks, own_index, axis)
            for step in range(1, size):
                target = lax.rem(own_index + step, size)
                part = pick(blocks, target, axis)
                total = total + shift(part, axis_name, size, step)
            return total

        parts = sum_small(parts, 2, "c", c_size, c_index)
        chip_parts = sum_small(parts, 1, "r", r_size, r_index)
        parts = z_sum(lambda step: pick(chip_parts, across(step), 0), f32)
        at = heads * piece
        q_bias_grad = parts[:at].reshape(heads, piece)
        v_bias_grad = parts[at : at + groups * piece].reshape(groups, piece)
        at = at + groups * piece
        k_bias_grad = parts[at : at + groups * HD].reshape(groups, HD)
        at = at + groups * HD
        gains = parts[at:].reshape(2, t_size, rows // t_size)
        gain_grads = sum_small(gains, 1, "tensor", t_size, t_index)
        return (
            hidden_out,
            input_grad,
            gain_grads[None],
            qkv_grad[None, :, :q_cols],
            qkv_grad[None, :, q_cols : q_cols + kv_cols],
            qkv_grad[None, :, q_cols + kv_cols :],
            o_grad[None],
            q_bias_grad[None],
            k_bias_grad[None],
            v_bias_grad[None],
            gate_grad[None],
            up_grad[None],
            down_grad[None],
        )

    return per_device


def solution(mesh):
    dp_size, t_size = mesh.shape["dp"], mesh.shape["tensor"]
    z_size, c_size = 4, 2
    r_size = dp_size // (z_size * c_size)
    fine = Mesh(
        mesh.devices.reshape(z_size, r_size, c_size, t_size), ("z", "r", "c", "tensor")
    )
    dp = ("z", "r", "c")
    every = ("z", "r", "c", "tensor")
    inner = make_step(z_size, r_size, c_size, t_size)

    return jax.shard_map(
        inner,
        mesh=fine,
        in_specs=(
            P(every, None),
            P(every, None),
            P(dp, None),
            P(dp, None),
            P(None, None, dp),
            P(None, dp, "tensor"),
            P(None, dp, "tensor"),
            P(None, dp, "tensor"),
            P(None, "tensor", dp),
            P(None, "tensor", dp),
            P(None, "tensor", dp),
            P(None, "tensor", dp),
            P(None, dp, "tensor"),
            P(None, dp, "tensor"),
            P(None, "tensor", dp),
        ),
        out_specs=(
            P(every, None),
            P(every, None),
            P(None, None, every),
            P(None, dp, "tensor"),
            P(None, dp, "tensor"),
            P(None, dp, "tensor"),
            P(None, "tensor", dp),
            P(None, "tensor", dp),
            P(None, "tensor", None),
            P(None, "tensor", dp),
            P(None, dp, "tensor"),
            P(None, dp, "tensor"),
            P(None, "tensor", dp),
        ),
        check_vma=False,
    )
```
